32 devices in a mesh: loss: 4 (over x, core), section: 2 (over y), mp: 4 (over z).
Axes of the slice: x: 2, y: 2, z: 4, core: 2. Of those that a mesh axis runs over, the one named last changes fastest.
Arguments:
- image_embed: bfloat16 [1024, 1152], P('loss'), may hold values from -0.1796875 to 0.1796875
- text_embed: bfloat16 [1024, 1152], P(('loss', 'section', 'mp')), may hold values from -0.1796875 to 0.1796875
- logit_scale: float32 [], replicated, may hold values from 4 to 16
- logit_bias: float32 [], replicated, may hold values from -3 to -1
Outputs:
- grad_image: float32 [1024, 1152], P(('loss', 'section', 'mp'))
- grad_text: float32 [1024, 1152], P(('loss', 'section', 'mp'))
The draws below stay inside these ranges and needn't reach their ends.
All inputs are finite; a program needn't handle non-finite values.
Results may differ from the reference program's by a relative error of at most 0.017.
Values may be sent and summed in bfloat16 or wider, within the bound.
No kernel may reach another device: no remote copies, remote signals or barrier semaphores. Data moves between devices by JAX's collectives and lax.ppermute only.
A program may use at most 64 MiB of HBM per device.

```python
import math
import jax
import jax.numpy as jnp
from jax import lax

E = 1152
PAIRS = 1024
N_LOSS = 4


def level_of(key, shape, pieces, low, top_value):
    factor_of = 1.0
    for axis_at, blocks in pieces:
        heights = jax.random.uniform(jax.random.fold_in(jax.random.fold_in(key, 6), axis_at), (blocks,), jnp.float32, low / len(pieces), top_value / len(pieces))
        factor_of = factor_of * jnp.repeat(jnp.exp(heights), shape[axis_at] // blocks).reshape((-1,) + (1,) * (len(shape) - 1 - axis_at))
    return factor_of


def normal_values(rng, shape, spread, reach, cuts=(), held_as=jnp.bfloat16):
    drawn = spread * jax.random.normal(rng, shape, jnp.float32)
    if cuts:
        drawn = drawn * level_of(rng, shape, cuts, -0.22, 0.18)
    return jnp.clip(drawn, -reach, reach).astype(held_as)


def setup_inputs(seed: int = 0) -> dict:
    keys = jax.random.split(jax.random.key(seed), 5)
    return {
        "image_embed": normal_values(keys[0], (PAIRS, E), 0.03, 0.1796875, ((0, 4),)),
        "text_embed": normal_values(keys[1], (PAIRS, E), 0.03, 0.1796875, ((0, 32),)),
        "logit_scale": jnp.clip(jnp.exp(jax.random.uniform(keys[2], (), jnp.float32, math.log(4.0), math.log(16.0))), 4.0, 16.0),
        "logit_bias": jnp.clip(jax.random.uniform(keys[3], (), jnp.float32, -3.0, -1.0), -3.0, -1.0),
    }


epsilon = 1e-06

def unit_rows(values):
    widened = values.astype(jnp.float32)
    scaling = lax.rsqrt(lax.optimization_barrier(jnp.sum(widened * widened, axis=-1, keepdims=True)) + epsilon)
    return (widened * scaling, scaling)

def unit_backward(unit, scaling, gradient):
    return (gradient - unit * lax.optimization_barrier(jnp.sum(unit * gradient, axis=-1, keepdims=True))) * scaling

def reference(image_embed, text_embed, logit_scale, logit_bias):
    unit_image, image_scaling = unit_rows(image_embed)
    unit_text, text_scaling = unit_rows(text_embed)
    image_low = unit_image.astype(jnp.bfloat16)
    text_low = unit_text.astype(jnp.bfloat16)
    pair_count = image_low.shape[0]
    width = image_low.shape[1]
    block_rows = pair_count // N_LOSS
    image_blocks = image_low.reshape(N_LOSS, block_rows, width)
    columns = jnp.arange(pair_count, dtype=jnp.int32)

    def visit(text_grad, scan_item):
        block_index, image_block = scan_item
        logits = logit_scale * jnp.dot(image_block, text_low.T, preferred_element_type=jnp.float32) + logit_bias
        row_ids = block_index * block_rows + jnp.arange(block_rows, dtype=jnp.int32)
        positive = (row_ids[:, None] == columns[None, :]).astype(jnp.float32)
        dlogit = (jax.nn.sigmoid(logits) - positive).astype(jnp.bfloat16)
        image_grad = logit_scale * jnp.dot(dlogit, text_low, preferred_element_type=jnp.float32)
        text_grad = text_grad + logit_scale * jnp.dot(dlogit.T, image_block, preferred_element_type=jnp.float32)
        return (text_grad, image_grad)
    start = jnp.zeros((pair_count, width), jnp.float32)
    text_grad, image_grads = lax.scan(visit, start, (jnp.arange(N_LOSS, dtype=jnp.int32), image_blocks))
    image_grad = image_grads.reshape(pair_count, width)
    grad_image = unit_backward(unit_image, image_scaling, image_grad)
    grad_text = unit_backward(unit_text, text_scaling, text_grad)
    return (grad_image, grad_text)
```

```python
import functools
import jax
import jax.numpy as jnp
from jax import lax
from jax.experimental import pallas as pl
from jax.experimental.pallas import tpu as pltpu
from jax.sharding import PartitionSpec as P

epsilon = 1e-06


def shifted(value, axis, steps):
    count = lax.axis_size(axis)
    pairs = [(source, (source + steps) % count) for source in range(count)]
    return lax.ppermute(value, axis, pairs)


def unit_rows(values):
    widened = values.astype(jnp.float32)
    scaling = lax.rsqrt(jnp.sum(widened * widened, axis=-1, keepdims=True) + epsilon)
    return (widened * scaling, scaling)


def unit_backward(unit, scaling, gradient):
    return (gradient - unit * jnp.sum(unit * gradient, axis=-1, keepdims=True)) * scaling


def row_scaling(values):
    widened = values.astype(jnp.float32)
    return lax.rsqrt(jnp.sum(widened * widened, axis=-1, keepdims=True) + epsilon)


def as_row(column):
    count = column.shape[0]
    rows = lax.broadcasted_iota(jnp.int32, (count, count), 0)
    cols = lax.broadcasted_iota(jnp.int32, (count, count), 1)
    return jnp.sum(jnp.where(rows == cols, column, 0.0), axis=0, keepdims=True)


def dot_last(left, right):
    return lax.dot_general(
        left, right, (((1,), (1,)), ((), ())), preferred_element_type=jnp.float32
    )


def text_kernel(n_texts, n_images, *refs):
    scale_ref, bias_ref = refs[:2]
    text_refs = refs[2 : 2 + n_texts]
    image_refs = refs[2 + n_texts : 2 + n_texts + n_images]
    out_refs = refs[2 + n_texts + n_images :]
    rows = text_refs[0].shape[0]
    group = lax.axis_index("section") * lax.axis_size("mp") + lax.axis_index("mp")
    texts = jnp.concatenate([ref[...] for ref in text_refs], axis=0)
    text_column = scale_ref[0] * row_scaling(texts)
    total = None
    for at, image_ref in enumerate(image_refs):
        images = image_ref[...]
        image_row = as_row(row_scaling(images))
        logits = dot_last(texts, images) * text_column * image_row + bias_ref[0]
        dlogit = jax.nn.sigmoid(logits)
        if at == 0:
            r = lax.broadcasted_iota(jnp.int32, dlogit.shape, 0)
            c = lax.broadcasted_iota(jnp.int32, dlogit.shape, 1)
            hit = (r < rows) & (c == r + group * rows)
            dlogit = dlogit - hit.astype(jnp.float32)
        part = jnp.dot(
            (dlogit * image_row).astype(jnp.bfloat16), images, preferred_element_type=jnp.float32
        )
        total = part if total is None else total + part
    for at, out_ref in enumerate(out_refs):
        out_ref[...] = total[at * rows : (at + 1) * rows].astype(out_ref.dtype)


def image_kernel(n_texts, scale_ref, bias_ref, image_ref, *refs):
    text_refs = refs[:n_texts]
    out_refs = refs[n_texts:]
    rows = text_refs[0].shape[0]
    n_mp = lax.axis_size("mp")
    mp = lax.axis_index("mp")
    first = lax.axis_index("section") * n_mp
    chunks = []
    for step in range(n_mp):
        start = (first + lax.bitwise_xor(mp, step)) * rows
        chunks.append(image_ref[pl.ds(pl.multiple_of(start, rows), rows), :])
    images = jnp.concatenate(chunks, axis=0)
    texts = jnp.concatenate([ref[...] for ref in text_refs], axis=0)
    image_column = scale_ref[0] * row_scaling(images)
    text_row = as_row(row_scaling(texts))
    logits = dot_last(images, texts) * image_column * text_row + bias_ref[0]
    dlogit = jax.nn.sigmoid(logits)
    r = lax.broadcasted_iota(jnp.int32, dlogit.shape, 0)
    c = lax.broadcasted_iota(jnp.int32, dlogit.shape, 1)
    hit = (r < rows) & (c == r)
    dlogit = dlogit - hit.astype(jnp.float32)
    total = jnp.dot(
        (dlogit * text_row).astype(jnp.bfloat16), texts, preferred_element_type=jnp.float32
    )
    for at, out_ref in enumerate(out_refs):
        out_ref[...] = total[at * rows : (at + 1) * rows].astype(out_ref.dtype)


def finish_kernel(pick, scale_ref, values_ref, *refs):
    part_refs, out_ref = refs[:-1], refs[-1]
    rows = out_ref.shape[0]
    if pick:
        group = lax.axis_index("section") * lax.axis_size("mp") + lax.axis_index("mp")
        values = values_ref[pl.ds(pl.multiple_of(group * rows, rows), rows), :]
    else:
        values = values_ref[...]
    unit, scaling = unit_rows(values)
    total = part_refs[0][...]
    for ref in part_refs[1:]:
        total = total + ref[...].astype(jnp.float32)
    out_ref[...] = unit_backward(unit, scaling, scale_ref[0] * total)


vmem = pl.BlockSpec(memory_space=pltpu.VMEM)
smem = pl.BlockSpec(memory_space=pltpu.SMEM)


def call(body, name, scalars, arrays, outs, flops):
    moved = sum(a.size * a.dtype.itemsize for a in arrays)
    return pl.pallas_call(
        body,
        name=name,
        out_shape=outs,
        in_specs=[smem] * len(scalars) + [vmem] * len(arrays),
        out_specs=jax.tree.map(lambda _: vmem, outs),
        cost_estimate=pl.CostEstimate(flops=flops, bytes_accessed=moved, transcendentals=0),
    )(*scalars, *arrays)


def few_devices(image_embed, text_embed, logit_scale, logit_bias):
    n_loss, n_section, n_mp = (lax.axis_size(a) for a in ("loss", "section", "mp"))
    rows, width = text_embed.shape
    scale = logit_scale.reshape(1)
    bias = logit_bias.reshape(1)

    def across(value, do, ds):
        pairs = [
            (l * n_section + s, (l ^ (2 * do)) * n_section + (s ^ ds))
            for l in range(n_loss)
            for s in range(n_section)
        ]
        return lax.ppermute(value, ("loss", "section"), pairs)

    def swapped(value):
        return lax.ppermute(value, "loss", [(l, l ^ 1) for l in range(n_loss)])

    n_outer = n_loss // 2
    peers = [(do, ds) for ds in range(n_section) for do in range(n_outer)]
    mine = {p: (text_embed if p == (0, 0) else across(text_embed, *p)) for p in peers}
    image_other = swapped(image_embed)
    other = {p: swapped(mine[p]) for p in peers}

    wide = jax.ShapeDtypeStruct((rows, width), jnp.float32)
    low = jax.ShapeDtypeStruct((rows, width), jnp.bfloat16)
    text_blocks = [mine[do, 0] for do in range(n_outer)]
    text_parts = call(
        functools.partial(text_kernel, n_outer, 2),
        "text_parts",
        (scale, bias),
        text_blocks + [image_embed, image_other],
        [wide] + [low] * (n_outer - 1),
        8 * n_outer * rows * image_embed.shape[0] * width,
    )
    text_back = [across(text_parts[do], do, 0) for do in range(1, n_outer)]

    blocks = [mine[p] for p in peers] + [other[p] for p in peers]
    image_parts = call(
        functools.partial(image_kernel, len(blocks)),
        "image_parts",
        (scale, bias),
        [image_embed] + blocks,
        [wide] + [low] * (n_mp - 1),
        4 * n_mp * rows * len(blocks) * rows * width,
    )
    image_back = [
        lax.ppermute(image_parts[step], "mp", [(i, i ^ step) for i in range(n_mp)])
        for step in reversed(range(1, n_mp))
    ]
    grad_text = call(
        functools.partial(finish_kernel, False),
        "finish_text",
        (scale,),
        [text_embed, text_parts[0]] + text_back,
        wide,
        1000,
    )
    grad_image = call(
        functools.partial(finish_kernel, True),
        "finish_image",
        (scale,),
        [image_embed, image_parts[0]] + image_back,
        wide,
        1000,
    )
    return (grad_image, grad_text)


def many_devices(image_embed, text_embed, logit_scale, logit_bias):
    unit_image, image_scaling = unit_rows(image_embed)
    unit_text, text_scaling = unit_rows(text_embed)
    image_low = unit_image.astype(jnp.bfloat16)
    text_low = unit_text.astype(jnp.bfloat16)
    image_rows = image_low.shape[0]
    text_rows = text_low.shape[0]
    width = image_low.shape[1]
    cycle_size = lax.axis_size("loss")
    group_index = lax.axis_index("section") * lax.axis_size("mp") + lax.axis_index("mp")
    group_offset = group_index * text_rows
    text_ids = jnp.arange(text_rows, dtype=jnp.int32)[:, None]
    image_cols = jnp.arange(image_rows, dtype=jnp.int32)[None, :] - group_offset
    diagonal = (text_ids == image_cols).astype(jnp.float32)

    def visit(stop_index, carried):
        block, text_grad, dlogit_stash, text_stash = carried
        logits = (
            logit_scale * jnp.dot(block, image_low.T, preferred_element_type=jnp.float32)
            + logit_bias
        )
        positive = jnp.where(stop_index == 0, diagonal, jnp.zeros_like(diagonal))
        dlogit = (jax.nn.sigmoid(logits) - positive).astype(jnp.bfloat16)
        text_grad = text_grad + logit_scale * jnp.dot(
            dlogit, image_low, preferred_element_type=jnp.float32
        )
        dlogit_stash = lax.dynamic_update_slice(dlogit_stash, dlogit[None], (stop_index, 0, 0))
        text_stash = lax.dynamic_update_slice(text_stash, block[None], (stop_index, 0, 0))
        block = shifted(block, "loss", 1)
        text_grad = shifted(text_grad, "loss", 1)
        return (block, text_grad, dlogit_stash, text_stash)

    start = (
        text_low,
        jnp.zeros((text_rows, width), jnp.float32),
        jnp.zeros((cycle_size, text_rows, image_rows), jnp.bfloat16),
        jnp.zeros((cycle_size, text_rows, width), jnp.bfloat16),
    )
    finished = lax.fori_loop(0, cycle_size, visit, start)
    text_grad = finished[1]
    dlogit_all = finished[2].reshape(cycle_size * text_rows, image_rows)
    texts_seen = finished[3].reshape(cycle_size * text_rows, width)
    image_grad = logit_scale * jnp.einsum(
        "ti,te->ie", dlogit_all, texts_seen, preferred_element_type=jnp.float32
    )
    image_share = lax.psum_scatter(
        image_grad.astype(jnp.bfloat16), ("section", "mp"), scatter_dimension=0, tiled=True
    ).astype(jnp.float32)
    own_unit = lax.dynamic_slice_in_dim(unit_image, group_offset, text_rows, 0)
    own_scaling = lax.dynamic_slice_in_dim(image_scaling, group_offset, text_rows, 0)
    grad_image = unit_backward(own_unit, own_scaling, image_share)
    grad_text = unit_backward(unit_text, text_scaling, text_grad)
    return (grad_image, grad_text)


def per_device(image_embed, text_embed, logit_scale, logit_bias):
    n_loss, n_section, n_mp = (lax.axis_size(a) for a in ("loss", "section", "mp"))
    paired = all(n & (n - 1) == 0 for n in (n_loss, n_section, n_mp)) and n_loss > 1
    if paired and n_loss * n_section <= 8 and n_mp <= 8:
        return few_devices(image_embed, text_embed, logit_scale, logit_bias)
    return many_devices(image_embed, text_embed, logit_scale, logit_bias)


def solution(mesh):
    placed = (P("loss", None), P(("loss", "section", "mp"), None), P(), P())
    return jax.shard_map(
        per_device,
        mesh=mesh,
        in_specs=placed,
        out_specs=(P(("loss", "section", "mp"), None), P(("loss", "section", "mp"), None)),
        check_vma=False,
    )
```
